32 devices in a mesh: groups: 2 (over y), ctx: 8 (over z, core), chan: 2 (over x).
Axes of the slice: x: 2, y: 2, z: 4, core: 2. Of those that a mesh axis runs over, the one named last changes fastest.
Arguments:
- tokens: bfloat16 [4096, 2048], P(('groups', 'ctx')), parts along dimension 0, may hold values from -6 to 6
- in_weight: bfloat16 [2048, 3, 2048], P('ctx', None, 'chan'), may hold values from -0.125 to 0.125
- short_taps: bfloat16 [3, 3, 2048], P(None, None, 'chan'), may hold values from -3.5 to 3.5
- filters: bfloat16 [2048, 2048], P('chan', 'ctx'), may hold values from -0.125 to 0.125
- doc_lengths: int32 [8], P('groups'), parts along dimension 0, may hold values from 1 to 1024, 2048 in all
- out_weight: bfloat16 [2048, 2048], P('chan', 'ctx'), may hold values from -0.125 to 0.125
Outputs:
- output: bfloat16 [4096, 2048], P(('groups', 'ctx', 'chan')), parts along dimension 0
The draws below stay inside these ranges and needn't reach their ends.
There are 2 independent parts, one for each index of `groups`. The reference program is written for one: setup_inputs(seed, part) draws one part's arguments, and reference() takes and returns one part's arrays. A program takes and returns all parts, laid end to end along the dimension named above; an argument that names none is the same for every part. Nothing has to cross between parts.
Inputs may be any that keep to these rules, and one draw needn't show every extreme that they name: doc_lengths are the lengths of the solutions packed one after another; they fill all 2048 positions.
All inputs are finite; a program needn't handle non-finite values.
Results may differ from the reference program's by a relative error of at most 0.007.
Values may be sent and summed in bfloat16 or wider, within the bound.
A program may use at most 64 MiB of HBM per device.

```python
import math
import jax
import jax.numpy as jnp
import numpy as np
from jax import lax

D = 2048
CH = 2048
SEQ = 2048
NDOCS = 4
MOST_LEN = 1024


def block_levels(own_key, shape, pieces, least, high):
    def one(dim, parts):
        heights = jax.random.uniform(jax.random.fold_in(jax.random.fold_in(own_key, 6), dim), (parts,), jnp.float32, least / len(pieces), high / len(pieces))
        return jnp.repeat(jnp.exp(heights), shape[dim] // parts).reshape((-1,) + (1,) * (len(shape) - dim - 1))

    gain = one(*pieces[0])
    for cut in pieces[1:]:
        gain = gain * one(*cut)
    return gain


def split_up(amount, total, most, lean):
    weights = [(1 << 20) // math.isqrt(grade ** lean) + 1 for grade in range(2, amount + 1)]
    rest, given = total - most - (amount - 1), [1] * (amount - 1)
    while rest > 0:
        free = [i for i in range(amount - 1) if given[i] < most]
        whole, budget = sum([weights[i] for i in free]), rest
        for i in free:
            addition = min(most - given[i], max(1, budget * weights[i] // whole), rest)
            given[i] = given[i] + addition
            rest = rest - addition
    return np.array([most] + given)


def ragged(rng, number_of, total, bound, slope):
    if number_of == 2:
        one = jax.random.randint(rng, (), max(1, total - bound), min(bound, total - 1) + 1)
        return jnp.stack([one, total - one])
    sizes = jnp.asarray(split_up(number_of, total, bound, slope), jnp.int32)
    pairs = (number_of - 1) // 2
    donor, receiver = sizes[1:1 + 2 * pairs:2], sizes[2:2 + 2 * pairs:2]
    margin = jnp.minimum(donor - 1, bound - receiver)
    passed = jax.random.randint(jax.random.fold_in(rng, 1), (pairs,), 0, 1 << 20) % (margin + 1)
    sizes = sizes.at[1:1 + 2 * pairs:2].set(donor - passed).at[2:2 + 2 * pairs:2].set(receiver + passed)
    return sizes[jax.random.permutation(jax.random.fold_in(rng, 2), number_of)]


def noise(rng, dims, scale, reach, split=(), kind=jnp.bfloat16):
    values = jax.random.normal(rng, dims, jnp.float32) * scale
    if len(split) > 0:
        values = block_levels(rng, dims, split, -0.22, 0.18) * values
    return jnp.clip(values, min=-reach, max=reach).astype(kind)


def setup_inputs(seed: int = 0, part: int = 0) -> dict:
    splits = jax.random.split(jax.random.key(seed), 7)
    own_keys = jax.random.split(jax.random.fold_in(splits[6], part), 7)
    return {
        "tokens": noise(own_keys[0], (SEQ, D), 1.0, 6.0, ((0, 8),)),
        "in_weight": noise(splits[1], (D, 3, CH), D ** -0.5, 0.125, ((0, 8), (2, 2))),
        "short_taps": noise(splits[2], (3, 3, CH), 3 ** -0.5, 3.5, ((2, 2),)),
        "filters": noise(splits[3], (CH, SEQ), SEQ ** -0.5, 0.125, ((0, 2), (1, 8))),
        "doc_lengths": ragged(own_keys[4], NDOCS, SEQ, MOST_LEN, 1).astype(jnp.int32),
        "out_weight": noise(splits[5], (CH, D), CH ** -0.5, 0.125, ((0, 2), (1, 8))),
    }


def document_ids(doc_lengths, seq_len):
    ends = jnp.cumsum(doc_lengths, dtype=jnp.int32)
    places = lax.broadcasted_iota(jnp.int32, (seq_len, ends.shape[0]), 0)
    return jnp.sum((places >= ends[None, :]).astype(jnp.int32), axis=1)


def short_conv(streams, taps, doc_id):
    result = taps[:, 0, :, None] * streams
    for lag in (1, 2):
        moved = jnp.pad(streams, ((0, 0), (0, 0), (lag, 0)))[:, :, :-lag]
        linked = jnp.concatenate((jnp.zeros((lag,), bool), doc_id[lag:] == doc_id[:-lag]))
        result = result + taps[:, lag, :, None] * jnp.where(linked[None, None, :], moved, 0.0)
    return result


def long_filter(gated, kernel):
    seq_len = gated.shape[-1]
    spectrum = jnp.fft.rfft(gated, n=2 * seq_len) * jnp.fft.rfft(kernel, n=2 * seq_len)
    return jnp.fft.irfft(spectrum, n=2 * seq_len)[..., :seq_len].astype(gated.dtype)


def reference(tokens, in_weight, short_taps, filters, doc_lengths, out_weight):
    seq_len = tokens.shape[0]
    doc_id = document_ids(doc_lengths, seq_len)
    block = math.gcd(CH, 256)
    tokens_wide = tokens.astype(jnp.float32)

    def one_block(index):
        offset = (index * block).astype(jnp.int32)
        weight = lax.dynamic_slice_in_dim(in_weight, offset, block, 2).astype(jnp.float32)
        streams = jnp.einsum("td,dsc->sct", tokens_wide, weight).astype(jnp.bfloat16)
        streams = lax.optimization_barrier(streams).astype(jnp.float32)
        taps = lax.dynamic_slice_in_dim(short_taps, offset, block, 2).astype(jnp.float32)
        conv = short_conv(streams, taps, doc_id)
        kernel = lax.dynamic_slice_in_dim(filters, offset, block, 0).astype(jnp.float32)
        filtered = long_filter(conv[0] * conv[2], kernel)
        return (conv[1] * filtered).astype(jnp.bfloat16)

    mixed = lax.map(one_block, jnp.arange(CH // block, dtype=jnp.int32)).reshape(CH, seq_len)
    output = lax.dot_general(mixed, out_weight, (((0,), (0,)), ((), ())), preferred_element_type=jnp.float32)
    return output.astype(jnp.bfloat16)
```

```python
import functools
import math

import jax
import jax.numpy as jnp
from jax import lax
from jax.experimental import pallas as pl
from jax.experimental.pallas import tpu as pltpu
from jax.sharding import PartitionSpec as P

def contract(form, left, right):
    return jnp.einsum(form, left, right, precision=lax.Precision.HIGHEST)


def angle_table(rows, cols, period):
    product = lax.broadcasted_iota(jnp.int32, (rows, cols), 0) * lax.broadcasted_iota(
        jnp.int32, (rows, cols), 1
    )
    theta = (product % period).astype(jnp.float32) * (2.0 * math.pi / period)
    return (jnp.cos(theta), jnp.sin(theta))


def document_ids(doc_lengths, seq_len):
    ends = jnp.cumsum(doc_lengths, dtype=jnp.int32)
    places = lax.broadcasted_iota(jnp.int32, (seq_len, ends.shape[0]), 0)
    return jnp.sum((places >= ends[None, :]).astype(jnp.int32), axis=1)


def short_conv(streams, taps, doc_id):
    result = taps[:, 0, :, None] * streams
    for lag in (1, 2):
        moved = jnp.pad(streams, ((0, 0), (0, 0), (lag, 0)))[:, :, :-lag]
        linked = jnp.concatenate((jnp.zeros((lag,), bool), doc_id[lag:] == doc_id[:-lag]))
        result = result + taps[:, lag, :, None] * jnp.where(linked[None, None, :], moved, 0.0)
    return result


def causal_filter(gated, kernel_rows):
    count, seq_len = gated.shape
    width = math.gcd(seq_len, 128)
    half = seq_len // width
    span = 2 * half
    total = span * width
    signal = gated.reshape(count, half, width)
    kernel = kernel_rows.reshape(count, half, width)
    cos_b, sin_b = angle_table(span, span, span)
    twist_c, twist_s = angle_table(span, width, total)
    cos_a, sin_a = angle_table(width, width, width)

    def forward(values):
        padded = jnp.concatenate((values, jnp.zeros_like(values)), 1)
        real_part = contract("kb,cba->cka", cos_b, padded)
        imag_part = -contract("kb,cba->cka", sin_b, padded)
        turned_r = real_part * twist_c + imag_part * twist_s
        turned_i = imag_part * twist_c - real_part * twist_s
        spec_r = contract("cka,aj->ckj", turned_r, cos_a) + contract("cka,aj->ckj", turned_i, sin_a)
        spec_i = contract("cka,aj->ckj", turned_i, cos_a) - contract("cka,aj->ckj", turned_r, sin_a)
        return (spec_r, spec_i)

    sig_r, sig_i = forward(signal)
    ker_r, ker_i = forward(kernel)
    prod_r = sig_r * ker_r - sig_i * ker_i
    prod_i = sig_r * ker_i + sig_i * ker_r
    back_r = contract("ckj,aj->cka", prod_r, cos_a) - contract("ckj,aj->cka", prod_i, sin_a)
    back_i = contract("ckj,aj->cka", prod_i, cos_a) + contract("ckj,aj->cka", prod_r, sin_a)
    untwist_r = back_r * twist_c - back_i * twist_s
    untwist_i = back_i * twist_c + back_r * twist_s
    blocks = contract("bk,cka->cba", cos_b, untwist_r) - contract("bk,cka->cba", sin_b, untwist_i)
    blocks = blocks[:, :half]
    return (blocks / total).reshape(count, seq_len)


def shards(tokens, in_weight, short_taps, filters, doc_lengths, out_weight):
    width_dev = in_weight.shape[2]
    group_width = width_dev // lax.axis_size("ctx")
    streams = jnp.einsum(
        "dsc,td->sct",
        lax.all_gather(in_weight, "ctx", axis=0, tiled=True),
        tokens,
        preferred_element_type=jnp.float32,
    )
    packed = jnp.concatenate((streams.astype(jnp.bfloat16), filters[None]), 0)
    spread = lax.all_to_all(packed, "ctx", split_axis=1, concat_axis=2, tiled=True)
    taps = lax.dynamic_slice_in_dim(
        short_taps, lax.axis_index("ctx") * group_width, group_width, 2
    ).astype(jnp.float32)
    seq_len = spread.shape[2]
    doc_id = document_ids(doc_lengths, seq_len)
    conv = short_conv(spread[:3].astype(jnp.float32), taps, doc_id)
    filtered = causal_filter(conv[0] * conv[2], spread[3].astype(jnp.float32))
    mixed = (conv[1] * filtered).astype(jnp.bfloat16)
    returned = lax.all_to_all(mixed, "ctx", split_axis=1, concat_axis=0, tiled=True)
    partial_out = lax.dot_general(
        returned,
        lax.all_gather(out_weight, "ctx", axis=1, tiled=True),
        (((0,), (0,)), ((), ())),
        preferred_element_type=jnp.float32,
    )
    return lax.psum_scatter(partial_out, "chan", scatter_dimension=0, tiled=True).astype(
        jnp.bfloat16
    )


TILE = 128
MESH = pl.DeviceIdType.MESH


def exchange_kernel(
    planes,
    packed_ref,
    tokens_ref,
    outw_ref,
    taps_ref,
    links_ref,
    out_ref,
    toks,
    wide,
    outw,
    streams,
    gated,
    kernels,
    bands,
    mixed,
    arrived,
    turned,
    own_part,
    sent_part,
    got_part,
    local_sem,
    tok_z_send,
    tok_z_recv,
    tok_x_send,
    tok_x_recv,
    tok_c_send,
    tok_c_recv,
    w_send,
    w_recv,
    w_y_send,
    w_y_recv,
    o_z_send,
    o_z_recv,
    o_y_send,
    o_y_recv,
    o_c_send,
    o_c_recv,
    m_send,
    m_recv,
    p_send,
    p_recv,
):
    g = lax.axis_index("groups")
    k = lax.axis_index("ctx")
    x = lax.axis_index("chan")
    z, core = k // 2, k % 2
    count = 2 * planes
    blocks = 2 * count
    lanes = tokens_ref.shape[0] // 2
    half_o = outw_ref.shape[0] // 2

    def at(group=g, ctx=k, chan=x):
        return (group, ctx, chan)

    def remote(src, dst, send, recv, where):
        return pltpu.make_async_remote_copy(
            src_ref=src,
            dst_ref=dst,
            send_sem=send,
            recv_sem=recv,
            device_id=where,
            device_id_type=MESH,
        )

    barrier = pltpu.get_barrier_semaphore()
    for step in range(1, count):
        pl.semaphore_signal(
            barrier, inc=1, device_id=at(ctx=(k + step) % count), device_id_type=MESH
        )
    pl.semaphore_signal(barrier, inc=1, device_id=at(chan=1 - x), device_id_type=MESH)
    pl.semaphore_signal(barrier, inc=1, device_id=at(group=1 - g), device_id_type=MESH)
    pl.semaphore_wait(barrier, count + 1)

    other = 2 * z + 1 - core

    def z_at(step):
        return 2 * ((z + step) % planes) + core

    def z_from(step):
        return 2 * ((z + planes - step) % planes) + core

    def tok(owner, half):
        return toks.at[owner, pl.ds(half * lanes, lanes), :]

    def column(owner, half):
        return wide.at[:, pl.ds(pl.multiple_of((2 * owner + half) * TILE, TILE), TILE)]

    def outw_at(owner, half):
        return outw.at[owner, pl.ds(half * half_o, half_o), :]

    waits = []

    locals_ = [
        pltpu.make_async_copy(tokens_ref, toks.at[k], local_sem.at[0]),
        pltpu.make_async_copy(packed_ref.at[k, 0], column(k, 0), local_sem.at[1]),
        pltpu.make_async_copy(packed_ref.at[k, 1], column(k, 1), local_sem.at[2]),
        pltpu.make_async_copy(outw_ref, outw.at[k], local_sem.at[3]),
    ]
    for copy in locals_:
        copy.start()

    w_copies = []
    for step in range(1, count):
        to = (k + step) % count
        copy = remote(
            packed_ref.at[to, g], column(k, g), w_send.at[step], w_recv.at[step], at(ctx=to)
        )
        copy.start()
        w_copies.append(copy)

    own_half = tokens_ref.at[pl.ds(x * lanes, lanes), :]
    tz_copies = []
    for step in range(1, planes):
        copy = remote(
            own_half, tok(k, x), tok_z_send.at[step], tok_z_recv.at[step], at(ctx=z_at(step))
        )
        copy.start()
        tz_copies.append(copy)
    copy = remote(tokens_ref, toks.at[k], tok_c_send.at[0], tok_c_recv.at[0], at(ctx=other))
    copy.start()
    waits.append(copy)

    for step in range(1, count):
        w_copies[step - 1].wait_recv()
        came = column((k + count - step) % count, g)
        copy = remote(came, came, w_y_send.at[step], w_y_recv.at[step], at(group=1 - g))
        copy.start()
        waits.append(copy)

    tx_copies = []
    for step in range(1, planes):
        tz_copies[step - 1].wait_recv()
        came = tok(z_from(step), x)
        copy = remote(came, came, tok_x_send.at[step], tok_x_recv.at[step], at(chan=1 - x))
        copy.start()
        tx_copies.append(copy)
        copy = remote(
            came, came, tok_c_send.at[2 * step - 1], tok_c_recv.at[2 * step - 1], at(ctx=other)
        )
        copy.start()
        waits.append(copy)

    own_o = outw_ref.at[pl.ds(g * half_o, half_o), :]
    oz_copies = []
    for step in range(1, planes):
        copy = remote(
            own_o, outw_at(k, g), o_z_send.at[step], o_z_recv.at[step], at(ctx=z_at(step))
        )
        copy.start()
        oz_copies.append(copy)
    oc_copies = []
    copy = remote(outw_ref, outw.at[k], o_c_send.at[0], o_c_recv.at[0], at(ctx=other))
    copy.start()
    oc_copies.append(copy)

    for step in range(1, planes):
        tx_copies[step - 1].wait_recv()
        came = tok(z_from(step), 1 - x)
        copy = remote(
            came, came, tok_c_send.at[2 * step], tok_c_recv.at[2 * step], at(ctx=other)
        )
        copy.start()
        waits.append(copy)
    for copy in locals_:
        copy.wait()
    for copy in waits:
        copy.wait_recv()
    for copy in w_copies + tz_copies + tx_copies + waits:
        copy.wait_send()

    rows = wide.shape[0]
    chans = rows // 4

    def project(index, carry):
        value = lax.dot_general(
            wide[: 3 * chans, :],
            toks[index],
            (((1,), (1,)), ((), ())),
            preferred_element_type=jnp.float32,
        )
        value = value.astype(jnp.bfloat16).astype(jnp.float32)
        streams[:, 2 * index, :] = value[:, :TILE]
        streams[:, 2 * index + 1, :] = value[:, TILE:]
        return carry

    lax.fori_loop(0, count, project, 0)
    for m in range(blocks):
        kernels[:, m, :] = wide[3 * chans :, m * TILE : (m + 1) * TILE].astype(jnp.float32)

    group = 8
    lane = lax.broadcasted_iota(jnp.int32, (group, blocks, TILE), 2)

    def short(index, carry):
        first = pl.multiple_of(index * group, group)
        results = []
        for s in range(3):
            value = streams[pl.ds(s * chans + first, group)]
            total = taps_ref[3 * s, pl.ds(first, group), :][:, None, :] * value
            for lag in (1, 2):
                rolled = pltpu.roll(value, lag, 2)
                moved = jnp.where(lane < lag, pltpu.roll(rolled, 1, 1), rolled)
                kept = jnp.where(links_ref[lag - 1][None] > 0.5, moved, 0.0)
                total = total + taps_ref[3 * s + lag, pl.ds(first, group), :][:, None, :] * kept
            results.append(total)
        gated[pl.ds(first, group), pl.ds(0, blocks), :] = jnp.zeros_like(results[0])
        gated[pl.ds(first, group), pl.ds(blocks, blocks), :] = results[0] * results[2]
        streams[pl.ds(chans + first, group)] = results[1]
        return carry

    lax.fori_loop(0, chans // group, short, 0)

    oy_copies = []
    for step in range(1, planes):
        oz_copies[step - 1].wait_recv()
        came = outw_at(z_from(step), g)
        copy = remote(came, came, o_y_send.at[step], o_y_recv.at[step], at(group=1 - g))
        copy.start()
        oy_copies.append(copy)
        copy = remote(
            came, came, o_c_send.at[2 * step - 1], o_c_recv.at[2 * step - 1], at(ctx=other)
        )
        copy.start()
        oc_copies.append(copy)

    ahead = lax.broadcasted_iota(jnp.int32, (TILE, TILE), 1) >= lax.broadcasted_iota(
        jnp.int32, (TILE, TILE), 0
    )

    def filter_pair(index, carry):
        lefts = []
        for u in range(2):
            c = 2 * index + u
            taps = kernels[c]
            before = jnp.zeros((TILE, TILE), jnp.float32)
            for m in range(blocks):
                row = jnp.broadcast_to(taps[m : m + 1, :], (TILE, TILE))
                turn = pltpu.roll(row, 0, 1, stride=1, stride_axis=0)
                bands[m * TILE : (m + 1) * TILE, u * TILE : (u + 1) * TILE] = jnp.where(
                    ahead, turn, before
                ).astype(jnp.bfloat16)
                before = turn
            lefts.append(
                jnp.concatenate(
                    [gated[c, pl.ds(blocks - m, blocks), :] for m in range(blocks)], axis=1
                ).astype(jnp.bfloat16)
            )
        value = jnp.dot(
            jnp.concatenate(lefts, axis=0), bands[...], preferred_element_type=jnp.float32
        )
        for u in range(2):
            c = 2 * index + u
            part = value[u * blocks : (u + 1) * blocks, u * TILE : (u + 1) * TILE]
            streams[chans + c] = streams[chans + c] * part
        return carry

    lax.fori_loop(0, chans // 2, filter_pair, 0)
    for m in range(blocks):
        mixed[m // 2, m % 2] = streams[pl.ds(chans, chans), m, :].astype(jnp.bfloat16)

    m_copies = []
    for step in range(1, count):
        to = (k + step) % count
        copy = remote(
            mixed.at[to], arrived.at[k], m_send.at[step], m_recv.at[step], at(ctx=to)
        )
        copy.start()
        m_copies.append(copy)
    own_mixed = pltpu.make_async_copy(mixed.at[k], arrived.at[k], local_sem.at[0])
    own_mixed.start()
    for step in range(1, planes):
        oy_copies[step - 1].wait_recv()
        came = outw_at(z_from(step), 1 - g)
        copy = remote(
            came, came, o_c_send.at[2 * step], o_c_recv.at[2 * step], at(ctx=other)
        )
        copy.start()
        oc_copies.append(copy)
    own_mixed.wait()
    for copy in m_copies:
        copy.wait_recv()
    for owner in range(count):
        for h in range(2):
            turned[h, :, owner * chans : (owner + 1) * chans] = (
                arrived[owner, h].astype(jnp.float32).T.astype(jnp.bfloat16)
            )
    for copy in oc_copies:
        copy.wait_recv()
    for copy in m_copies + oz_copies + oy_copies + oc_copies:
        copy.wait_send()

    wide_e = outw_ref.shape[1]
    for owner in range(count):
        sent_part[:, owner * wide_e : (owner + 1) * wide_e] = jnp.dot(
            turned[1 - x], outw[owner], preferred_element_type=jnp.float32
        ).astype(jnp.bfloat16)
    copy = remote(sent_part, got_part, p_send.at[0], p_recv.at[0], at(chan=1 - x))
    copy.start()
    for owner in range(count):
        own_part[:, owner * wide_e : (owner + 1) * wide_e] = jnp.dot(
            turned[x], outw[owner], preferred_element_type=jnp.float32
        )
    copy.wait()
    out_ref[...] = (own_part[...] + got_part[...].astype(jnp.float32)).astype(jnp.bfloat16)


def fused(tokens, in_weight, short_taps, filters, doc_lengths, out_weight):
    count = lax.axis_size("ctx")
    depth = in_weight.shape[0]
    chans = in_weight.shape[2] // count
    span = filters.shape[1]
    rows, model = tokens.shape
    seq_len = span * count
    blocks = seq_len // TILE
    weights = in_weight.reshape(2, depth // 2, 3, count, chans).transpose(3, 0, 2, 4, 1)
    weights = weights.reshape(count, 2, 3 * chans, depth // 2)
    lags = filters.reshape(count, chans, 2, span // 2).transpose(0, 2, 1, 3)
    packed = jnp.concatenate((weights, lags), 2)
    taps = lax.dynamic_slice_in_dim(short_taps, lax.axis_index("ctx") * chans, chans, 2)
    taps = jnp.broadcast_to(
        taps.astype(jnp.float32).reshape(9, chans)[:, :, None], (9, chans, TILE)
    )
    doc_id = document_ids(doc_lengths, seq_len)
    links = []
    for lag in (1, 2):
        links.append(jnp.concatenate((jnp.zeros((lag,), bool), doc_id[lag:] == doc_id[:-lag])))
    links = jnp.stack(links).astype(jnp.float32).reshape(2, blocks, TILE)

    planes = count // 2
    dma = pltpu.SemaphoreType.DMA
    anywhere = pl.BlockSpec(memory_space=pl.ANY)
    vmem = pl.BlockSpec(memory_space=pltpu.VMEM)
    return pl.pallas_call(
        functools.partial(exchange_kernel, planes),
        out_shape=jax.ShapeDtypeStruct((rows // 2, model), jnp.bfloat16),
        in_specs=[anywhere, anywhere, anywhere, vmem, vmem],
        out_specs=vmem,
        scratch_shapes=[
            pltpu.VMEM((count, rows, model), jnp.bfloat16),
            pltpu.VMEM((4 * chans, model), jnp.bfloat16),
            pltpu.VMEM((count, out_weight.shape[0], out_weight.shape[1]), jnp.bfloat16),
            pltpu.VMEM((3 * chans, blocks, TILE), jnp.float32),
            pltpu.VMEM((chans, 2 * blocks, TILE), jnp.float32),
            pltpu.VMEM((chans, blocks, TILE), jnp.float32),
            pltpu.VMEM((seq_len, 2 * TILE), jnp.bfloat16),
            pltpu.VMEM((count, 2, chans, TILE), jnp.bfloat16),
            pltpu.VMEM((count, 2, chans, TILE), jnp.bfloat16),
            pltpu.VMEM((2, TILE, count * chans), jnp.bfloat16),
            pltpu.VMEM((TILE, model), jnp.float32),
            pltpu.VMEM((TILE, model), jnp.bfloat16),
            pltpu.VMEM((TILE, model), jnp.bfloat16),
            dma((4,)),
        ]
        + [dma((planes,))] * 4
        + [dma((2 * planes - 1,))] * 2
        + [dma((count,))] * 4
        + [dma((planes,))] * 4
        + [dma((2 * planes - 1,))] * 2
        + [dma((count,))] * 2
        + [dma((1,))] * 2,
        compiler_params=pltpu.CompilerParams(
            collective_id=0, has_side_effects=True, vmem_limit_bytes=56 * 1024 * 1024
        ),
    )(packed, tokens, out_weight, taps, links)


def fits(tokens, in_weight, filters, out_weight):
    count = lax.axis_size("ctx")
    rows, model = tokens.shape
    return (
        count % 2 == 0
        and lax.axis_size("chan") == 2
        and lax.axis_size("groups") == 2
        and in_weight.shape[0] == 2 * TILE
        and in_weight.shape[2] == count * TILE
        and filters.shape[1] == 2 * TILE
        and rows == 2 * TILE
        and out_weight.shape[1] * count == model
        and count * rows * model * 2 <= 16 * 1024 * 1024
    )


def layer(tokens, in_weight, short_taps, filters, doc_lengths, out_weight):
    if fits(tokens, in_weight, filters, out_weight):
        return fused(tokens, in_weight, short_taps, filters, doc_lengths, out_weight)
    return shards(tokens, in_weight, short_taps, filters, doc_lengths, out_weight)


def solution(mesh):
    placed = (
        P(("groups", "ctx"), None),
        P("ctx", None, "chan"),
        P(None, None, "chan"),
        P("chan", "ctx"),
        P("groups"),
        P("chan", "ctx"),
    )
    return jax.shard_map(
        layer,
        mesh=mesh,
        in_specs=placed,
        out_specs=P(("groups", "ctx", "chan"), None),
        check_vma=False,
    )
```

```python
import functools
import math

import jax
import jax.numpy as jnp
from jax import lax
from jax.experimental import pallas as pl
from jax.experimental.pallas import tpu as pltpu
from jax.sharding import PartitionSpec as P

def contract(form, left, right):
    return jnp.einsum(form, left, right, precision=lax.Precision.HIGHEST)


def angle_table(rows, cols, period):
    product = lax.broadcasted_iota(jnp.int32, (rows, cols), 0) * lax.broadcasted_iota(
        jnp.int32, (rows, cols), 1
    )
    theta = (product % period).astype(jnp.float32) * (2.0 * math.pi / period)
    return (jnp.cos(theta), jnp.sin(theta))


def document_ids(doc_lengths, seq_len):
    ends = jnp.cumsum(doc_lengths, dtype=jnp.int32)
    places = lax.broadcasted_iota(jnp.int32, (seq_len, ends.shape[0]), 0)
    return jnp.sum((places >= ends[None, :]).astype(jnp.int32), axis=1)


def short_conv(streams, taps, doc_id):
    result = taps[:, 0, :, None] * streams
    for lag in (1, 2):
        moved = jnp.pad(streams, ((0, 0), (0, 0), (lag, 0)))[:, :, :-lag]
        linked = jnp.concatenate((jnp.zeros((lag,), bool), doc_id[lag:] == doc_id[:-lag]))
        result = result + taps[:, lag, :, None] * jnp.where(linked[None, None, :], moved, 0.0)
    return result


def causal_filter(gated, kernel_rows):
    count, seq_len = gated.shape
    width = math.gcd(seq_len, 128)
    half = seq_len // width
    span = 2 * half
    total = span * width
    signal = gated.reshape(count, half, width)
    kernel = kernel_rows.reshape(count, half, width)
    cos_b, sin_b = angle_table(span, span, span)
    twist_c, twist_s = angle_table(span, width, total)
    cos_a, sin_a = angle_table(width, width, width)

    def forward(values):
        padded = jnp.concatenate((values, jnp.zeros_like(values)), 1)
        real_part = contract("kb,cba->cka", cos_b, padded)
        imag_part = -contract("kb,cba->cka", sin_b, padded)
        turned_r = real_part * twist_c + imag_part * twist_s
        turned_i = imag_part * twist_c - real_part * twist_s
        spec_r = contract("cka,aj->ckj", turned_r, cos_a) + contract("cka,aj->ckj", turned_i, sin_a)
        spec_i = contract("cka,aj->ckj", turned_i, cos_a) - contract("cka,aj->ckj", turned_r, sin_a)
        return (spec_r, spec_i)

    sig_r, sig_i = forward(signal)
    ker_r, ker_i = forward(kernel)
    prod_r = sig_r * ker_r - sig_i * ker_i
    prod_i = sig_r * ker_i + sig_i * ker_r
    back_r = contract("ckj,aj->cka", prod_r, cos_a) - contract("ckj,aj->cka", prod_i, sin_a)
    back_i = contract("ckj,aj->cka", prod_i, cos_a) + contract("ckj,aj->cka", prod_r, sin_a)
    untwist_r = back_r * twist_c - back_i * twist_s
    untwist_i = back_i * twist_c + back_r * twist_s
    blocks = contract("bk,cka->cba", cos_b, untwist_r) - contract("bk,cka->cba", sin_b, untwist_i)
    blocks = blocks[:, :half]
    return (blocks / total).reshape(count, seq_len)


def shards(tokens, in_weight, short_taps, filters, doc_lengths, out_weight):
    width_dev = in_weight.shape[2]
    group_width = width_dev // lax.axis_size("ctx")
    streams = jnp.einsum(
        "dsc,td->sct",
        lax.all_gather(in_weight, "ctx", axis=0, tiled=True),
        tokens,
        preferred_element_type=jnp.float32,
    )
    packed = jnp.concatenate((streams.astype(jnp.bfloat16), filters[None]), 0)
    spread = lax.all_to_all(packed, "ctx", split_axis=1, concat_axis=2, tiled=True)
    taps = lax.dynamic_slice_in_dim(
        short_taps, lax.axis_index("ctx") * group_width, group_width, 2
    ).astype(jnp.float32)
    seq_len = spread.shape[2]
    doc_id = document_ids(doc_lengths, seq_len)
    conv = short_conv(spread[:3].astype(jnp.float32), taps, doc_id)
    filtered = causal_filter(conv[0] * conv[2], spread[3].astype(jnp.float32))
    mixed = (conv[1] * filtered).astype(jnp.bfloat16)
    returned = lax.all_to_all(mixed, "ctx", split_axis=1, concat_axis=0, tiled=True)
    partial_out = lax.dot_general(
        returned,
        lax.all_gather(out_weight, "ctx", axis=1, tiled=True),
        (((0,), (0,)), ((), ())),
        preferred_element_type=jnp.float32,
    )
    return lax.psum_scatter(partial_out, "chan", scatter_dimension=0, tiled=True).astype(
        jnp.bfloat16
    )


TILE = 128
MESH = pl.DeviceIdType.MESH


def exchange_kernel(
    planes,
    packed_ref,
    tokens_ref,
    outw_ref,
    taps_ref,
    links_ref,
    out_ref,
    toks,
    wide,
    outw,
    streams,
    gated,
    kernels,
    bands,
    mixed,
    arrived,
    turned,
    own_part,
    sent_part,
    got_part,
    local_sem,
    own_send,
    own_recv,
    tok_z_send,
    tok_z_recv,
    tok_x_send,
    tok_x_recv,
    tok_c_send,
    tok_c_recv,
    w_send,
    w_recv,
    w_y_send,
    w_y_recv,
    o_z_send,
    o_z_recv,
    o_y_send,
    o_y_recv,
    o_c_send,
    o_c_recv,
    m_send,
    m_recv,
    p_send,
    p_recv,
):
    g = lax.axis_index("groups")
    k = lax.axis_index("ctx")
    x = lax.axis_index("chan")
    z, core = k // 2, k % 2
    count = 2 * planes
    blocks = 2 * count
    lanes = tokens_ref.shape[0] // 2
    half_o = outw_ref.shape[0] // 2

    def at(group=g, ctx=k, chan=x):
        return (group, ctx, chan)

    def remote(src, dst, send, recv, where):
        return pltpu.make_async_remote_copy(
            src_ref=src,
            dst_ref=dst,
            send_sem=send,
            recv_sem=recv,
            device_id=where,
            device_id_type=MESH,
        )

    barrier = pltpu.get_barrier_semaphore()
    for step in range(1, count):
        pl.semaphore_signal(
            barrier, inc=1, device_id=at(ctx=(k + step) % count), device_id_type=MESH
        )
    pl.semaphore_signal(barrier, inc=1, device_id=at(chan=1 - x), device_id_type=MESH)
    pl.semaphore_signal(barrier, inc=1, device_id=at(group=1 - g), device_id_type=MESH)
    pl.semaphore_wait(barrier, count + 1)

    other = 2 * z + 1 - core

    def tok(owner, half):
        return toks.at[owner, pl.ds(half * lanes, lanes), :]

    def column(owner, half):
        return wide.at[:, pl.ds(pl.multiple_of((2 * owner + half) * TILE, TILE), TILE)]

    def outw_at(owner, half):
        return outw.at[owner, pl.ds(half * half_o, half_o), :]

    waits = []

    locals_ = [
        pltpu.make_async_copy(tokens_ref, toks.at[k], local_sem.at[0]),
        pltpu.make_async_copy(packed_ref.at[k, 0], column(k, 0), local_sem.at[1]),
        pltpu.make_async_copy(packed_ref.at[k, 1], column(k, 1), local_sem.at[2]),
        pltpu.make_async_copy(outw_ref, outw.at[k], local_sem.at[3]),
    ]
    for copy in locals_:
        copy.start()

    w_copies = []
    for step in range(1, count):
        to = (k + step) % count
        copy = remote(
            packed_ref.at[to, g], column(k, g), w_send.at[step], w_recv.at[step], at(ctx=to)
        )
        copy.start()
        w_copies.append(copy)

    sends = []

    def present(side, step):
        return z >= step if side == 0 else z + step < planes

    def onward(side):
        return z + 1 < planes if side == 0 else z >= 1

    def origin(side, step):
        return 2 * (z - step if side == 0 else z + step) + core

    def beyond(side):
        return at(ctx=2 * (z + 1 if side == 0 else z - 1) + core)

    def hop(side, step, src, block, send, recv):
        def copy():
            return remote(
                src(side, step), block(side, step), send.at[side, step], recv.at[side, step], beyond(side)
            )

        ready = onward(side)
        if step > 1:
            ready = jnp.logical_and(ready, present(side, step - 1))

        @pl.when(ready)
        def _():
            copy().start()

        sends.append((ready, copy))

    def when(condition, action):
        pl.when(condition)(action)

    def tok_here(side, step, half):
        return tok(origin(side, step), half)

    own_half = tokens_ref.at[pl.ds(x * lanes, lanes), :]

    def tok_src(side, step):
        return own_half if step == 1 else tok_here(side, step - 1, x)

    def tok_dst(side, step):
        return tok_here(side, step - 1, x)

    for side in range(2):
        hop(side, 1, tok_src, tok_dst, tok_z_send, tok_z_recv)
    core_own = remote(tokens_ref, toks.at[k], own_send.at[0], own_recv.at[0], at(ctx=other))
    core_own.start()

    for step in range(1, count):
        w_copies[step - 1].wait_recv()
        came = column((k + count - step) % count, g)
        copy = remote(came, came, w_y_send.at[step], w_y_recv.at[step], at(group=1 - g))
        copy.start()
        waits.append(copy)

    def tok_z(side, step):
        came = tok_here(side, step, x)
        return remote(
            came, came, tok_z_send.at[side, step], tok_z_recv.at[side, step], at(ctx=other)
        )

    def tok_x(side, step, half):
        came = tok_here(side, step, half)
        return remote(
            came, came, tok_x_send.at[side, step], tok_x_recv.at[side, step], at(chan=1 - x)
        )

    def tok_c(side, step, half, which):
        came = tok_here(side, step, half)
        return remote(
            came,
            came,
            tok_c_send.at[which, side, step],
            tok_c_recv.at[which, side, step],
            at(ctx=other),
        )

    for step in range(1, planes):
        for side in range(2):

            def arrive(side=side, step=step):
                tok_z(side, step).wait_recv()
                tok_x(side, step, x).start()
                tok_c(side, step, x, 0).start()

            when(present(side, step), arrive)
            if step + 1 < planes:
                hop(side, step + 1, tok_src, tok_dst, tok_z_send, tok_z_recv)

    own_o = outw_ref.at[pl.ds(g * half_o, half_o), :]

    def outw_here(side, step, half):
        return outw_at(origin(side, step), half)

    def outw_src(side, step):
        return own_o if step == 1 else outw_here(side, step - 1, g)

    def outw_dst(side, step):
        return outw_here(side, step - 1, g)

    for side in range(2):
        hop(side, 1, outw_src, outw_dst, o_z_send, o_z_recv)
    core_own_o = remote(outw_ref, outw.at[k], own_send.at[1], own_recv.at[1], at(ctx=other))
    core_own_o.start()

    for step in range(1, planes):
        for side in range(2):

            def arrive_x(side=side, step=step):
                tok_x(side, step, 1 - x).wait_recv()
                tok_c(side, step, 1 - x, 1).start()

            when(present(side, step), arrive_x)
    for copy in locals_:
        copy.wait()
    for copy in waits:
        copy.wait_recv()
    core_own.wait_recv()
    for step in range(1, planes):
        for side in range(2):

            def arrive_c(side=side, step=step):
                for which in range(2):
                    tok_c(side, step, which, which).wait_recv()

            when(present(side, step), arrive_c)

    rows = wide.shape[0]
    chans = rows // 4

    def project(index, carry):
        value = lax.dot_general(
            wide[: 3 * chans, :],
            toks[index],
            (((1,), (1,)), ((), ())),
            preferred_element_type=jnp.float32,
        )
        value = value.astype(jnp.bfloat16).astype(jnp.float32)
        streams[:, 2 * index, :] = value[:, :TILE]
        streams[:, 2 * index + 1, :] = value[:, TILE:]
        return carry

    lax.fori_loop(0, count, project, 0)
    kernels[...] = wide[3 * chans :, :].astype(jnp.float32)

    group = 8
    lane = lax.broadcasted_iota(jnp.int32, (group, blocks, TILE), 2)

    def short(index, carry):
        first = pl.multiple_of(index * group, group)
        results = []
        for s in range(3):
            value = streams[pl.ds(s * chans + first, group)]
            total = taps_ref[3 * s, pl.ds(first, group), :][:, None, :] * value
            for lag in (1, 2):
                rolled = pltpu.roll(value, lag, 2)
                moved = jnp.where(lane < lag, pltpu.roll(rolled, 1, 1), rolled)
                kept = jnp.where(links_ref[lag - 1][None] > 0.5, moved, 0.0)
                total = total + taps_ref[3 * s + lag, pl.ds(first, group), :][:, None, :] * kept
            results.append(total)
        gated[pl.ds(first, group), pl.ds(0, blocks), :] = jnp.zeros_like(results[0])
        gated[pl.ds(first, group), pl.ds(blocks, blocks), :] = results[0] * results[2]
        streams[pl.ds(chans + first, group)] = results[1]
        return carry

    lax.fori_loop(0, chans // group, short, 0)

    def outw_z(side, step):
        came = outw_here(side, step, g)
        return remote(
            came, came, o_z_send.at[side, step], o_z_recv.at[side, step], at(ctx=other)
        )

    def outw_y(side, step, half):
        came = outw_here(side, step, half)
        return remote(
            came, came, o_y_send.at[side, step], o_y_recv.at[side, step], at(group=1 - g)
        )

    def outw_c(side, step, half, which):
        came = outw_here(side, step, half)
        return remote(
            came, came, o_c_send.at[which, side, step], o_c_recv.at[which, side, step], at(ctx=other)
        )

    def outw_step(step):
        for side in range(2):

            def arrive(side=side):
                outw_z(side, step).wait_recv()
                outw_y(side, step, g).start()
                outw_c(side, step, g, 0).start()

            when(present(side, step), arrive)
            if step + 1 < planes:
                hop(side, step + 1, outw_src, outw_dst, o_z_send, o_z_recv)

    def outw_last(step):
        for side in range(2):

            def arrive(side=side):
                outw_y(side, step, 1 - g).wait_recv()
                outw_c(side, step, 1 - g, 1).start()

            when(present(side, step), arrive)

    thick = 16
    place = lax.broadcasted_iota(jnp.int32, (thick, TILE), 1) - lax.broadcasted_iota(
        jnp.int32, (thick, TILE), 0
    )

    def filter_pair(index, carry):
        lefts = []
        for u in range(2):
            c = 2 * index + u
            taps = jnp.broadcast_to(kernels[pl.ds(c, 1), :], (thick, blocks * TILE))
            base = pltpu.roll(taps, 0, 1, stride=1, stride_axis=0).astype(jnp.bfloat16)
            for q in range(TILE // thick):
                moved = base if q == 0 else pltpu.roll(base, q * thick, 1)
                for m in range(blocks):
                    tile = moved[:, m * TILE : (m + 1) * TILE]
                    if m == 0:
                        tile = jnp.where(place >= q * thick, tile.astype(jnp.float32), 0.0).astype(
                            jnp.bfloat16
                        )
                    bands[
                        m * TILE + q * thick : m * TILE + (q + 1) * thick,
                        u * TILE : (u + 1) * TILE,
                    ] = tile
            lefts.append(
                jnp.concatenate(
                    [gated[c, pl.ds(blocks - m, blocks), :] for m in range(blocks)], axis=1
                ).astype(jnp.bfloat16)
            )
        value = jnp.dot(
            jnp.concatenate(lefts, axis=0), bands[...], preferred_element_type=jnp.float32
        )
        for u in range(2):
            c = 2 * index + u
            part = value[u * blocks : (u + 1) * blocks, u * TILE : (u + 1) * TILE]
            streams[chans + c] = streams[chans + c] * part
        return carry

    parts = 4
    size = chans // parts
    m_copies = []
    for part in range(parts):
        lax.fori_loop(part * size // 2, (part + 1) * size // 2, filter_pair, 0)
        first = part * size
        for m in range(blocks):
            mixed[m // 2, m % 2, first : first + size, :] = streams[
                chans + first : chans + first + size, m, :
            ].astype(jnp.bfloat16)
        for step in range(1, count):
            to = (k + step) % count
            copy = remote(
                mixed.at[to, :, pl.ds(first, size), :],
                arrived.at[k, :, pl.ds(first, size), :],
                m_send.at[part, step],
                m_recv.at[part, step],
                at(ctx=to),
            )
            copy.start()
            m_copies.append(copy)
        if part + 1 < planes:
            outw_step(part + 1)
    for step in range(parts, planes):
        outw_step(step)
    for step in range(1, planes):
        outw_last(step)
    own_mixed = pltpu.make_async_copy(mixed.at[k], arrived.at[k], local_sem.at[0])
    own_mixed.start()
    own_mixed.wait()
    for copy in m_copies:
        copy.wait_recv()
    for owner in range(count):
        for h in range(2):
            turned[h, :, owner * chans : (owner + 1) * chans] = (
                arrived[owner, h].astype(jnp.float32).T.astype(jnp.bfloat16)
            )
    core_own_o.wait_recv()
    for step in range(1, planes):
        for side in range(2):

            def arrive_oc(side=side, step=step):
                for which in range(2):
                    outw_c(side, step, which, which).wait_recv()

            when(present(side, step), arrive_oc)

    wide_e = outw_ref.shape[1]
    p_copies = []
    for owner in range(count):
        sent_part[owner] = jnp.dot(
            turned[1 - x], outw[owner], preferred_element_type=jnp.float32
        ).astype(jnp.bfloat16)
        copy = remote(
            sent_part.at[owner], got_part.at[owner], p_send.at[owner], p_recv.at[owner], at(chan=1 - x)
        )
        copy.start()
        p_copies.append(copy)
    for owner in range(count):
        span = slice(owner * wide_e, (owner + 1) * wide_e)
        own_part[:, span] = jnp.dot(
            turned[x], outw[owner], preferred_element_type=jnp.float32
        )
    for owner in range(count):
        span = slice(owner * wide_e, (owner + 1) * wide_e)
        p_copies[owner].wait_recv()
        out_ref[:, span] = (own_part[:, span] + got_part[owner].astype(jnp.float32)).astype(
            jnp.bfloat16
        )

    for copy in w_copies + waits + m_copies + p_copies:
        copy.wait_send()
    core_own.wait_send()
    core_own_o.wait_send()
    for ready, copy in sends:

        def left(copy=copy):
            copy().wait_send()

        when(ready, left)
    for step in range(1, planes):
        for side in range(2):

            def gone(side=side, step=step):
                tok_x(side, step, x).wait_send()
                tok_c(side, step, x, 0).wait_send()
                tok_c(side, step, 1 - x, 1).wait_send()
                outw_y(side, step, g).wait_send()
                outw_c(side, step, g, 0).wait_send()
                outw_c(side, step, 1 - g, 1).wait_send()

            when(present(side, step), gone)


def fused(tokens, in_weight, short_taps, filters, doc_lengths, out_weight):
    count = lax.axis_size("ctx")
    depth = in_weight.shape[0]
    chans = in_weight.shape[2] // count
    span = filters.shape[1]
    rows, model = tokens.shape
    seq_len = span * count
    blocks = seq_len // TILE
    weights = in_weight.reshape(2, depth // 2, 3, count, chans).transpose(3, 0, 2, 4, 1)
    weights = weights.reshape(count, 2, 3 * chans, depth // 2)
    lags = filters.reshape(count, chans, 2, span // 2).transpose(0, 2, 1, 3)
    packed = jnp.concatenate((weights, lags), 2)
    taps = lax.dynamic_slice_in_dim(short_taps, lax.axis_index("ctx") * chans, chans, 2)
    taps = jnp.broadcast_to(
        taps.astype(jnp.float32).reshape(9, chans)[:, :, None], (9, chans, TILE)
    )
    doc_id = document_ids(doc_lengths, seq_len)
    links = []
    for lag in (1, 2):
        links.append(jnp.concatenate((jnp.zeros((lag,), bool), doc_id[lag:] == doc_id[:-lag])))
    links = jnp.stack(links).astype(jnp.float32).reshape(2, blocks, TILE)

    planes = count // 2
    dma = pltpu.SemaphoreType.DMA
    anywhere = pl.BlockSpec(memory_space=pl.ANY)
    vmem = pl.BlockSpec(memory_space=pltpu.VMEM)
    return pl.pallas_call(
        functools.partial(exchange_kernel, planes),
        out_shape=jax.ShapeDtypeStruct((rows // 2, model), jnp.bfloat16),
        in_specs=[anywhere, anywhere, anywhere, vmem, vmem],
        out_specs=vmem,
        scratch_shapes=[
            pltpu.VMEM((count, rows, model), jnp.bfloat16),
            pltpu.VMEM((4 * chans, model), jnp.bfloat16),
            pltpu.VMEM((count, out_weight.shape[0], out_weight.shape[1]), jnp.bfloat16),
            pltpu.VMEM((3 * chans, blocks, TILE), jnp.float32),
            pltpu.VMEM((chans, 2 * blocks, TILE), jnp.float32),
            pltpu.VMEM((chans, seq_len), jnp.float32),
            pltpu.VMEM((seq_len, 2 * TILE), jnp.bfloat16),
            pltpu.VMEM((count, 2, chans, TILE), jnp.bfloat16),
            pltpu.VMEM((count, 2, chans, TILE), jnp.bfloat16),
            pltpu.VMEM((2, TILE, count * chans), jnp.bfloat16),
            pltpu.VMEM((TILE, model), jnp.float32),
            pltpu.VMEM((count, TILE, out_weight.shape[1]), jnp.bfloat16),
            pltpu.VMEM((count, TILE, out_weight.shape[1]), jnp.bfloat16),
            dma((4,)),
            dma((2,)),
            dma((2,)),
        ]
        + [dma((2, planes))] * 4
        + [dma((2, 2, planes))] * 2
        + [dma((count,))] * 4
        + [dma((2, planes))] * 4
        + [dma((2, 2, planes))] * 2
        + [dma((4, count))] * 2
        + [dma((count,))] * 2,
        compiler_params=pltpu.CompilerParams(
            collective_id=0, has_side_effects=True, vmem_limit_bytes=56 * 1024 * 1024
        ),
    )(packed, tokens, out_weight, taps, links)


def fits(tokens, in_weight, filters, out_weight):
    count = lax.axis_size("ctx")
    rows, model = tokens.shape
    return (
        count % 2 == 0
        and lax.axis_size("chan") == 2
        and lax.axis_size("groups") == 2
        and in_weight.shape[0] == 2 * TILE
        and in_weight.shape[2] == count * TILE
        and filters.shape[1] == 2 * TILE
        and rows == 2 * TILE
        and out_weight.shape[1] * count == model
        and count * rows * model * 2 <= 16 * 1024 * 1024
    )


def layer(tokens, in_weight, short_taps, filters, doc_lengths, out_weight):
    if fits(tokens, in_weight, filters, out_weight):
        return fused(tokens, in_weight, short_taps, filters, doc_lengths, out_weight)
    return shards(tokens, in_weight, short_taps, filters, doc_lengths, out_weight)


def solution(mesh):
    placed = (
        P(("groups", "ctx"), None),
        P("ctx", None, "chan"),
        P(None, None, "chan"),
        P("chan", "ctx"),
        P("groups"),
        P("chan", "ctx"),
    )
    return jax.shard_map(
        layer,
        mesh=mesh,
        in_specs=placed,
        out_specs=P(("groups", "ctx", "chan"), None),
        check_vma=False,
    )
```

```python
import functools
import math

import jax
import jax.numpy as jnp
from jax import lax
from jax.experimental import pallas as pl
from jax.experimental.pallas import tpu as pltpu
from jax.sharding import PartitionSpec as P

def contract(form, left, right):
    return jnp.einsum(form, left, right, precision=lax.Precision.HIGHEST)


def angle_table(rows, cols, period):
    product = lax.broadcasted_iota(jnp.int32, (rows, cols), 0) * lax.broadcasted_iota(
        jnp.int32, (rows, cols), 1
    )
    theta = (product % period).astype(jnp.float32) * (2.0 * math.pi / period)
    return (jnp.cos(theta), jnp.sin(theta))


def document_ids(doc_lengths, seq_len):
    ends = jnp.cumsum(doc_lengths, dtype=jnp.int32)
    places = lax.broadcasted_iota(jnp.int32, (seq_len, ends.shape[0]), 0)
    return jnp.sum((places >= ends[None, :]).astype(jnp.int32), axis=1)


def short_conv(streams, taps, doc_id):
    result = taps[:, 0, :, None] * streams
    for lag in (1, 2):
        moved = jnp.pad(streams, ((0, 0), (0, 0), (lag, 0)))[:, :, :-lag]
        linked = jnp.concatenate((jnp.zeros((lag,), bool), doc_id[lag:] == doc_id[:-lag]))
        result = result + taps[:, lag, :, None] * jnp.where(linked[None, None, :], moved, 0.0)
    return result


def causal_filter(gated, kernel_rows):
    count, seq_len = gated.shape
    width = math.gcd(seq_len, 128)
    half = seq_len // width
    span = 2 * half
    total = span * width
    signal = gated.reshape(count, half, width)
    kernel = kernel_rows.reshape(count, half, width)
    cos_b, sin_b = angle_table(span, span, span)
    twist_c, twist_s = angle_table(span, width, total)
    cos_a, sin_a = angle_table(width, width, width)

    def forward(values):
        padded = jnp.concatenate((values, jnp.zeros_like(values)), 1)
        real_part = contract("kb,cba->cka", cos_b, padded)
        imag_part = -contract("kb,cba->cka", sin_b, padded)
        turned_r = real_part * twist_c + imag_part * twist_s
        turned_i = imag_part * twist_c - real_part * twist_s
        spec_r = contract("cka,aj->ckj", turned_r, cos_a) + contract("cka,aj->ckj", turned_i, sin_a)
        spec_i = contract("cka,aj->ckj", turned_i, cos_a) - contract("cka,aj->ckj", turned_r, sin_a)
        return (spec_r, spec_i)

    sig_r, sig_i = forward(signal)
    ker_r, ker_i = forward(kernel)
    prod_r = sig_r * ker_r - sig_i * ker_i
    prod_i = sig_r * ker_i + sig_i * ker_r
    back_r = contract("ckj,aj->cka", prod_r, cos_a) - contract("ckj,aj->cka", prod_i, sin_a)
    back_i = contract("ckj,aj->cka", prod_i, cos_a) + contract("ckj,aj->cka", prod_r, sin_a)
    untwist_r = back_r * twist_c - back_i * twist_s
    untwist_i = back_i * twist_c + back_r * twist_s
    blocks = contract("bk,cka->cba", cos_b, untwist_r) - contract("bk,cka->cba", sin_b, untwist_i)
    blocks = blocks[:, :half]
    return (blocks / total).reshape(count, seq_len)


def shards(tokens, in_weight, short_taps, filters, doc_lengths, out_weight):
    width_dev = in_weight.shape[2]
    group_width = width_dev // lax.axis_size("ctx")
    streams = jnp.einsum(
        "dsc,td->sct",
        lax.all_gather(in_weight, "ctx", axis=0, tiled=True),
        tokens,
        preferred_element_type=jnp.float32,
    )
    packed = jnp.concatenate((streams.astype(jnp.bfloat16), filters[None]), 0)
    spread = lax.all_to_all(packed, "ctx", split_axis=1, concat_axis=2, tiled=True)
    taps = lax.dynamic_slice_in_dim(
        short_taps, lax.axis_index("ctx") * group_width, group_width, 2
    ).astype(jnp.float32)
    seq_len = spread.shape[2]
    doc_id = document_ids(doc_lengths, seq_len)
    conv = short_conv(spread[:3].astype(jnp.float32), taps, doc_id)
    filtered = causal_filter(conv[0] * conv[2], spread[3].astype(jnp.float32))
    mixed = (conv[1] * filtered).astype(jnp.bfloat16)
    returned = lax.all_to_all(mixed, "ctx", split_axis=1, concat_axis=0, tiled=True)
    partial_out = lax.dot_general(
        returned,
        lax.all_gather(out_weight, "ctx", axis=1, tiled=True),
        (((0,), (0,)), ((), ())),
        preferred_element_type=jnp.float32,
    )
    return lax.psum_scatter(partial_out, "chan", scatter_dimension=0, tiled=True).astype(
        jnp.bfloat16
    )


TILE = 128
MESH = pl.DeviceIdType.MESH


def exchange_kernel(
    planes,
    packed_ref,
    filters_ref,
    tokens_ref,
    outw_ref,
    taps_ref,
    links_ref,
    out_ref,
    toks,
    wide,
    outw,
    streams,
    gated,
    kernels,
    bands,
    early,
    mixed,
    arrived,
    turned,
    own_part,
    sent_part,
    got_part,
    local_sem,
    own_send,
    own_recv,
    tok_z_send,
    tok_z_recv,
    tok_x_send,
    tok_x_recv,
    tok_c_send,
    tok_c_recv,
    w_send,
    w_recv,
    w_y_send,
    w_y_recv,
    f_send,
    f_recv,
    f_y_send,
    f_y_recv,
    o_z_send,
    o_z_recv,
    o_y_send,
    o_y_recv,
    o_c_send,
    o_c_recv,
    m_send,
    m_recv,
    p_send,
    p_recv,
):
    g = lax.axis_index("groups")
    k = lax.axis_index("ctx")
    x = lax.axis_index("chan")
    z, core = k // 2, k % 2
    count = 2 * planes
    blocks = 2 * count
    lanes = tokens_ref.shape[0] // 2
    half_o = outw_ref.shape[0] // 2

    def at(group=g, ctx=k, chan=x):
        return (group, ctx, chan)

    def remote(src, dst, send, recv, where):
        return pltpu.make_async_remote_copy(
            src_ref=src,
            dst_ref=dst,
            send_sem=send,
            recv_sem=recv,
            device_id=where,
            device_id_type=MESH,
        )

    barrier = pltpu.get_barrier_semaphore()
    for step in range(1, count):
        pl.semaphore_signal(
            barrier, inc=1, device_id=at(ctx=(k + step) % count), device_id_type=MESH
        )
    pl.semaphore_signal(barrier, inc=1, device_id=at(chan=1 - x), device_id_type=MESH)
    pl.semaphore_signal(barrier, inc=1, device_id=at(group=1 - g), device_id_type=MESH)
    pl.semaphore_wait(barrier, count + 1)

    other = 2 * z + 1 - core

    def tok(owner, half):
        return toks.at[owner, pl.ds(half * lanes, lanes), :]

    depth3 = packed_ref.shape[2]

    def tile_of(index):
        return pl.ds(pl.multiple_of(index * TILE, TILE), TILE)

    def column(owner, half):
        return wide.at[pl.ds(0, depth3), tile_of(2 * owner + half)]

    def lag_column(owner, half):
        return wide.at[pl.ds(depth3, TILE), tile_of(2 * owner + half)]

    def lags_of(owner, half):
        return filters_ref.at[tile_of(owner), tile_of(half)]

    def outw_at(owner, half):
        return outw.at[owner, pl.ds(half * half_o, half_o), :]

    waits = []

    locals_ = [
        pltpu.make_async_copy(tokens_ref, toks.at[k], local_sem.at[0]),
        pltpu.make_async_copy(packed_ref.at[k, 0], column(k, 0), local_sem.at[1]),
        pltpu.make_async_copy(packed_ref.at[k, 1], column(k, 1), local_sem.at[2]),
        pltpu.make_async_copy(outw_ref, outw.at[k], local_sem.at[3]),
        pltpu.make_async_copy(lags_of(k, 0), lag_column(k, 0), local_sem.at[4]),
        pltpu.make_async_copy(lags_of(k, 1), lag_column(k, 1), local_sem.at[5]),
    ]
    for copy in locals_:
        copy.start()

    f_copies = []
    for step in range(1, count):
        to = (k + step) % count
        copy = remote(
            lags_of(to, g), lag_column(k, g), f_send.at[step], f_recv.at[step], at(ctx=to)
        )
        copy.start()
        f_copies.append(copy)

    sends = []

    def present(side, step):
        return z >= step if side == 0 else z + step < planes

    def onward(side):
        return z + 1 < planes if side == 0 else z >= 1

    def origin(side, step):
        return 2 * (z - step if side == 0 else z + step) + core

    def beyond(side):
        return at(ctx=2 * (z + 1 if side == 0 else z - 1) + core)

    def hop(side, step, src, block, send, recv):
        def copy():
            return remote(
                src(side, step), block(side, step), send.at[side, step], recv.at[side, step], beyond(side)
            )

        ready = onward(side)
        if step > 1:
            ready = jnp.logical_and(ready, present(side, step - 1))

        @pl.when(ready)
        def _():
            copy().start()

        sends.append((ready, copy))

    def when(condition, action):
        pl.when(condition)(action)

    def tok_here(side, step, half):
        return tok(origin(side, step), half)

    own_half = tokens_ref.at[pl.ds(x * lanes, lanes), :]

    def tok_src(side, step):
        return own_half if step == 1 else tok_here(side, step - 1, x)

    def tok_dst(side, step):
        return tok_here(side, step - 1, x)

    for side in range(2):
        hop(side, 1, tok_src, tok_dst, tok_z_send, tok_z_recv)
    core_own = remote(tokens_ref, toks.at[k], own_send.at[0], own_recv.at[0], at(ctx=other))
    core_own.start()

    w_copies = []
    for step in range(1, count):
        to = (k + step) % count
        copy = remote(
            packed_ref.at[to, g], column(k, g), w_send.at[step], w_recv.at[step], at(ctx=to)
        )
        copy.start()
        w_copies.append(copy)
    fy_copies = []
    for step in range(1, count):
        f_copies[step - 1].wait_recv()
        came = lag_column((k + count - step) % count, g)
        copy = remote(came, came, f_y_send.at[step], f_y_recv.at[step], at(group=1 - g))
        copy.start()
        fy_copies.append(copy)

    for step in range(1, count):
        w_copies[step - 1].wait_recv()
        came = column((k + count - step) % count, g)
        copy = remote(came, came, w_y_send.at[step], w_y_recv.at[step], at(group=1 - g))
        copy.start()
        waits.append(copy)

    thick = 16
    place = lax.broadcasted_iota(jnp.int32, (thick, TILE), 1) - lax.broadcasted_iota(
        jnp.int32, (thick, TILE), 0
    )

    def build(index, band):
        for u in range(2):
            taps = jnp.broadcast_to(
                kernels[pl.ds(2 * index + u, 1), :], (thick, blocks * TILE)
            )
            base = pltpu.roll(taps, 0, 1, stride=1, stride_axis=0).astype(jnp.bfloat16)
            for q in range(TILE // thick):
                moved = base if q == 0 else pltpu.roll(base, q * thick, 1)
                for m in range(blocks):
                    tile = moved[:, m * TILE : (m + 1) * TILE]
                    if m == 0:
                        tile = jnp.where(place >= q * thick, tile.astype(jnp.float32), 0.0).astype(
                            jnp.bfloat16
                        )
                    band[
                        m * TILE + q * thick : m * TILE + (q + 1) * thick,
                        u * TILE : (u + 1) * TILE,
                    ] = tile

    def build_early(index, carry):
        build(index, early.at[index])
        return carry

    for copy in fy_copies:
        copy.wait_recv()
    for copy in locals_[4:]:
        copy.wait()
    kernels[...] = wide[depth3:, :].astype(jnp.float32)
    ahead = early.shape[0] // (planes - 1)

    def tok_z(side, step):
        came = tok_here(side, step, x)
        return remote(
            came, came, tok_z_send.at[side, step], tok_z_recv.at[side, step], at(ctx=other)
        )

    def tok_x(side, step, half):
        came = tok_here(side, step, half)
        return remote(
            came, came, tok_x_send.at[side, step], tok_x_recv.at[side, step], at(chan=1 - x)
        )

    def tok_c(side, step, half, which):
        came = tok_here(side, step, half)
        return remote(
            came,
            came,
            tok_c_send.at[which, side, step],
            tok_c_recv.at[which, side, step],
            at(ctx=other),
        )

    for step in range(1, planes):
        for side in range(2):

            def arrive(side=side, step=step):
                tok_z(side, step).wait_recv()
                tok_x(side, step, x).start()
                tok_c(side, step, x, 0).start()

            when(present(side, step), arrive)
            if step + 1 < planes:
                hop(side, step + 1, tok_src, tok_dst, tok_z_send, tok_z_recv)
        last = early.shape[0] if step == planes - 1 else step * ahead
        lax.fori_loop((step - 1) * ahead, last, build_early, 0)

    own_o = outw_ref.at[pl.ds(g * half_o, half_o), :]

    def outw_here(side, step, half):
        return outw_at(origin(side, step), half)

    def outw_src(side, step):
        return own_o if step == 1 else outw_here(side, step - 1, g)

    def outw_dst(side, step):
        return outw_here(side, step - 1, g)

    for side in range(2):
        hop(side, 1, outw_src, outw_dst, o_z_send, o_z_recv)
    core_own_o = remote(outw_ref, outw.at[k], own_send.at[1], own_recv.at[1], at(ctx=other))
    core_own_o.start()

    for step in range(1, planes):
        for side in range(2):

            def arrive_x(side=side, step=step):
                tok_x(side, step, 1 - x).wait_recv()
                tok_c(side, step, 1 - x, 1).start()

            when(present(side, step), arrive_x)
    def outw_z(side, step):
        came = outw_here(side, step, g)
        return remote(
            came, came, o_z_send.at[side, step], o_z_recv.at[side, step], at(ctx=other)
        )

    def outw_y(side, step, half):
        came = outw_here(side, step, half)
        return remote(
            came, came, o_y_send.at[side, step], o_y_recv.at[side, step], at(group=1 - g)
        )

    def outw_c(side, step, half, which):
        came = outw_here(side, step, half)
        return remote(
            came, came, o_c_send.at[which, side, step], o_c_recv.at[which, side, step], at(ctx=other)
        )

    def outw_step(step):
        for side in range(2):

            def arrive(side=side):
                outw_z(side, step).wait_recv()
                outw_y(side, step, g).start()
                outw_c(side, step, g, 0).start()

            when(present(side, step), arrive)
            if step + 1 < planes:
                hop(side, step + 1, outw_src, outw_dst, o_z_send, o_z_recv)

    def outw_last(step):
        for side in range(2):

            def arrive(side=side):
                outw_y(side, step, 1 - g).wait_recv()
                outw_c(side, step, 1 - g, 1).start()

            when(present(side, step), arrive)

    outw_step(1)
    for copy in locals_[:4]:
        copy.wait()
    for copy in waits:
        copy.wait_recv()
    core_own.wait_recv()
    for step in range(1, planes):
        for side in range(2):

            def arrive_c(side=side, step=step):
                for which in range(2):
                    tok_c(side, step, which, which).wait_recv()

            when(present(side, step), arrive_c)

    rows = wide.shape[0]
    chans = rows // 4

    def project(index, carry):
        value = lax.dot_general(
            wide[: 3 * chans, :],
            toks[index],
            (((1,), (1,)), ((), ())),
            preferred_element_type=jnp.float32,
        )
        value = value.astype(jnp.bfloat16).astype(jnp.float32)
        streams[:, 2 * index, :] = value[:, :TILE]
        streams[:, 2 * index + 1, :] = value[:, TILE:]
        return carry

    lax.fori_loop(0, count, project, 0)
    if planes > 2:
        outw_step(2)

    group = 8
    lane = lax.broadcasted_iota(jnp.int32, (group, blocks, TILE), 2)

    def short(index, carry):
        first = pl.multiple_of(index * group, group)
        results = []
        for s in range(3):
            value = streams[pl.ds(s * chans + first, group)]
            total = taps_ref[3 * s, pl.ds(first, group), :][:, None, :] * value
            for lag in (1, 2):
                rolled = pltpu.roll(value, lag, 2)
                moved = jnp.where(lane < lag, pltpu.roll(rolled, 1, 1), rolled)
                kept = jnp.where(links_ref[lag - 1][None] > 0.5, moved, 0.0)
                total = total + taps_ref[3 * s + lag, pl.ds(first, group), :][:, None, :] * kept
            results.append(total)
        gated[pl.ds(first, group), pl.ds(0, blocks), :] = jnp.zeros_like(results[0])
        gated[pl.ds(first, group), pl.ds(blocks, blocks), :] = results[0] * results[2]
        streams[pl.ds(chans + first, group)] = results[1]
        return carry

    lax.fori_loop(0, chans // group, short, 0)
    for step in range(3, planes):
        outw_step(step)

    def filter_pair(index, band):
        lefts = []
        for u in range(2):
            lefts.append(
                jnp.concatenate(
                    [
                        gated[2 * index + u, pl.ds(blocks - m, blocks), :]
                        for m in range(blocks)
                    ],
                    axis=1,
                ).astype(jnp.bfloat16)
            )
        value = jnp.dot(
            jnp.concatenate(lefts, axis=0), band[...], preferred_element_type=jnp.float32
        )
        for u in range(2):
            c = 2 * index + u
            part = value[u * blocks : (u + 1) * blocks, u * TILE : (u + 1) * TILE]
            streams[chans + c] = streams[chans + c] * part

    def filter_early(index, carry):
        for slot in range(2):
            filter_pair(2 * index + slot, early.at[2 * index + slot])
        return carry

    def filter_quad(index, carry):
        for slot in range(2):
            build(2 * index + slot, bands.at[slot])
            filter_pair(2 * index + slot, bands.at[slot])
        return carry

    parts = 4
    size = chans // parts
    m_copies = []
    for part in range(parts):
        begin, end = part * size // 4, (part + 1) * size // 4
        middle = min(max(begin, early.shape[0] // 2), end)
        lax.fori_loop(begin, middle, filter_early, 0)
        lax.fori_loop(middle, end, filter_quad, 0)
        first = part * size
        for m in range(blocks):
            mixed[m // 2, m % 2, first : first + size, :] = streams[
                chans + first : chans + first + size, m, :
            ].astype(jnp.bfloat16)
        for step in range(1, count):
            to = (k + step) % count
            copy = remote(
                mixed.at[to, :, pl.ds(first, size), :],
                arrived.at[k, :, pl.ds(first, size), :],
                m_send.at[part, step],
                m_recv.at[part, step],
                at(ctx=to),
            )
            copy.start()
            m_copies.append(copy)
        if part == 1:
            for step in range(1, planes):
                outw_last(step)
    own_mixed = pltpu.make_async_copy(mixed.at[k], arrived.at[k], local_sem.at[0])
    own_mixed.start()
    own_mixed.wait()
    for copy in m_copies:
        copy.wait_recv()
    for owner in range(count):
        for h in range(2):
            turned[h, :, owner * chans : (owner + 1) * chans] = (
                arrived[owner, h].astype(jnp.float32).T.astype(jnp.bfloat16)
            )
    core_own_o.wait_recv()
    for step in range(1, planes):
        for side in range(2):

            def arrive_oc(side=side, step=step):
                for which in range(2):
                    outw_c(side, step, which, which).wait_recv()

            when(present(side, step), arrive_oc)

    wide_e = outw_ref.shape[1]
    p_copies = []
    for owner in range(count):
        sent_part[owner] = jnp.dot(
            turned[1 - x], outw[owner], preferred_element_type=jnp.float32
        ).astype(jnp.bfloat16)
        copy = remote(
            sent_part.at[owner], got_part.at[owner], p_send.at[owner], p_recv.at[owner], at(chan=1 - x)
        )
        copy.start()
        p_copies.append(copy)
    for owner in range(count):
        span = slice(owner * wide_e, (owner + 1) * wide_e)
        own_part[:, span] = jnp.dot(
            turned[x], outw[owner], preferred_element_type=jnp.float32
        )
    for owner in range(count):
        span = slice(owner * wide_e, (owner + 1) * wide_e)
        p_copies[owner].wait_recv()
        out_ref[:, span] = (own_part[:, span] + got_part[owner].astype(jnp.float32)).astype(
            jnp.bfloat16
        )

    for copy in w_copies + f_copies + fy_copies + waits + m_copies + p_copies:
        copy.wait_send()
    core_own.wait_send()
    core_own_o.wait_send()
    for ready, copy in sends:

        def left(copy=copy):
            copy().wait_send()

        when(ready, left)
    for step in range(1, planes):
        for side in range(2):

            def gone(side=side, step=step):
                tok_x(side, step, x).wait_send()
                tok_c(side, step, x, 0).wait_send()
                tok_c(side, step, 1 - x, 1).wait_send()
                outw_y(side, step, g).wait_send()
                outw_c(side, step, g, 0).wait_send()
                outw_c(side, step, 1 - g, 1).wait_send()

            when(present(side, step), gone)


def fused(tokens, in_weight, short_taps, filters, doc_lengths, out_weight):
    count = lax.axis_size("ctx")
    depth = in_weight.shape[0]
    chans = in_weight.shape[2] // count
    rows, model = tokens.shape
    seq_len = filters.shape[1] * count
    blocks = seq_len // TILE
    weights = in_weight.reshape(2, depth // 2, 3, count, chans).transpose(3, 0, 2, 4, 1)
    packed = weights.reshape(count, 2, 3 * chans, depth // 2)
    taps = lax.dynamic_slice_in_dim(short_taps, lax.axis_index("ctx") * chans, chans, 2)
    taps = jnp.broadcast_to(
        taps.astype(jnp.float32).reshape(9, chans)[:, :, None], (9, chans, TILE)
    )
    doc_id = document_ids(doc_lengths, seq_len)
    links = []
    for lag in (1, 2):
        links.append(jnp.concatenate((jnp.zeros((lag,), bool), doc_id[lag:] == doc_id[:-lag])))
    links = jnp.stack(links).astype(jnp.float32).reshape(2, blocks, TILE)

    planes = count // 2
    dma = pltpu.SemaphoreType.DMA
    anywhere = pl.BlockSpec(memory_space=pl.ANY)
    vmem = pl.BlockSpec(memory_space=pltpu.VMEM)
    return pl.pallas_call(
        functools.partial(exchange_kernel, planes),
        out_shape=jax.ShapeDtypeStruct((rows // 2, model), jnp.bfloat16),
        in_specs=[anywhere] * 4 + [vmem, vmem],
        out_specs=vmem,
        scratch_shapes=[
            pltpu.VMEM((count, rows, model), jnp.bfloat16),
            pltpu.VMEM((4 * chans, model), jnp.bfloat16),
            pltpu.VMEM((count, out_weight.shape[0], out_weight.shape[1]), jnp.bfloat16),
            pltpu.VMEM((3 * chans, blocks, TILE), jnp.float32),
            pltpu.VMEM((chans, 2 * blocks, TILE), jnp.float32),
            pltpu.VMEM((chans, seq_len), jnp.float32),
            pltpu.VMEM((2, seq_len, 2 * TILE), jnp.bfloat16),
            pltpu.VMEM((24, seq_len, 2 * TILE), jnp.bfloat16),
            pltpu.VMEM((count, 2, chans, TILE), jnp.bfloat16),
            pltpu.VMEM((count, 2, chans, TILE), jnp.bfloat16),
            pltpu.VMEM((2, TILE, count * chans), jnp.bfloat16),
            pltpu.VMEM((TILE, model), jnp.float32),
            pltpu.VMEM((count, TILE, out_weight.shape[1]), jnp.bfloat16),
            pltpu.VMEM((count, TILE, out_weight.shape[1]), jnp.bfloat16),
            dma((6,)),
            dma((2,)),
            dma((2,)),
        ]
        + [dma((2, planes))] * 4
        + [dma((2, 2, planes))] * 2
        + [dma((count,))] * 8
        + [dma((2, planes))] * 4
        + [dma((2, 2, planes))] * 2
        + [dma((4, count))] * 2
        + [dma((count,))] * 2,
        compiler_params=pltpu.CompilerParams(
            collective_id=0, has_side_effects=True, vmem_limit_bytes=60 * 1024 * 1024
        ),
    )(packed, filters, tokens, out_weight, taps, links)


def fits(tokens, in_weight, filters, out_weight):
    count = lax.axis_size("ctx")
    rows, model = tokens.shape
    return (
        count % 2 == 0
        and lax.axis_size("chan") == 2
        and lax.axis_size("groups") == 2
        and in_weight.shape[0] == 2 * TILE
        and in_weight.shape[2] == count * TILE
        and filters.shape[1] == 2 * TILE
        and rows == 2 * TILE
        and out_weight.shape[1] * count == model
        and count * rows * model * 2 <= 16 * 1024 * 1024
    )


def layer(tokens, in_weight, short_taps, filters, doc_lengths, out_weight):
    if fits(tokens, in_weight, filters, out_weight):
        return fused(tokens, in_weight, short_taps, filters, doc_lengths, out_weight)
    return shards(tokens, in_weight, short_taps, filters, doc_lengths, out_weight)


def solution(mesh):
    placed = (
        P(("groups", "ctx"), None),
        P("ctx", None, "chan"),
        P(None, None, "chan"),
        P("chan", "ctx"),
        P("groups"),
        P("chan", "ctx"),
    )
    return jax.shard_map(
        layer,
        mesh=mesh,
        in_specs=placed,
        out_specs=P(("groups", "ctx", "chan"), None),
        check_vma=False,
    )
```
